32 devices in a mesh: term: 8 (over z, y), sec: 4 (over x, core).
Axes of the slice: x: 2, y: 2, z: 4, core: 2. Of those that a mesh axis runs over, the one named last changes fastest.
Arguments:
- state: bfloat16 [4, 768, 768], P('sec'), may hold values from -6 to 6
- left_environment: bfloat16 [8, 4, 768, 768], P('term', 'sec'), may hold values from -0.21875 to 0.21875
- right_environment: bfloat16 [8, 4, 768, 768], P('term', 'sec'), may hold values from -0.21875 to 0.21875
- site_blocks: bfloat16 [4, 768, 768], P('sec'), may hold values from -3 to 3
- sector_sizes: int32 [4], replicated, may hold values from 192 to 768, as said below
- term_shift: int32 [8], P('term'), may hold values from -1 to 1
Outputs:
- applied: float32 [4, 768, 768], P('sec', 'term')
- new_left: bfloat16 [8, 4, 768, 768], P('term', 'sec')
The draws below stay inside these ranges and needn't reach their ends.
Inputs may be any that keep to these rules, and one draw needn't show every extreme that they name: `sector_sizes`: every sector holds at least 192 states and the largest sector holds exactly 768.
All inputs are finite; a program needn't handle non-finite values.
Results may differ from the reference program's by a relative error of at most 0.0049.
Values may be sent and summed in bfloat16 or wider, within the bound.
A program may use at most 64 MiB of HBM per device.

```python
import jax
import jax.numpy as jnp
from jax import lax

M = 768
NSEC = 4
NTERM = 8


def draw_sector_sizes(key, part):
    first_key, second_key = jax.random.split(jax.random.fold_in(key, 11))
    counts = jax.random.randint(first_key, (NSEC,), M // 4, M + 1)
    largest = jax.random.randint(second_key, (), 0, NSEC)
    return counts.at[largest].set(M).astype(jnp.int32)


def touch_ends(entries, stream_key, least, top_value):
    longest = entries.shape.index(max(entries.shape))
    spots = []
    for shift in (0, 1):
        where = [jax.random.randint(jax.random.fold_in(stream_key, axis), (), 0, length) for axis, length in enumerate(entries.shape)]
        where[longest] = (where[longest] + shift) % entries.shape[longest]
        spots.append(tuple(where))
    return entries.at[spots[0]].set(least).at[spots[1]].set(top_value)


def block_levels(stream_key, dims, cuts, least, high):
    loudness, own = 1.0, jax.random.fold_in(stream_key, 6)
    for dim, blocks in cuts:
        steps = jnp.exp(jax.random.uniform(jax.random.fold_in(own, dim), (blocks,), jnp.float32, least / len(cuts), high / len(cuts)))
        loudness = loudness * jnp.repeat(steps, dims[dim] // blocks).reshape([-1 if axis == dim else 1 for axis in range(len(dims))])
    return loudness


def noise(key, shape, width, most, cuts=(), held_as=jnp.bfloat16):
    level = block_levels(key, shape, cuts, -0.22, 0.18) if cuts else 1.0
    values = jax.random.normal(key, shape, jnp.float32) * width * level
    return jnp.minimum(jnp.maximum(values, -most), most).astype(held_as)


def setup_inputs(seed: int = 0) -> dict:
    streams_of = jax.random.split(jax.random.key(seed), 7)
    return {
        "state": noise(streams_of[0], (NSEC, M, M), 1.0, 6.0, ((0, 4),)),
        "left_environment": noise(streams_of[1], (NTERM, NSEC, M, M), M ** -0.5, 0.21875, ((0, 8), (1, 4))),
        "right_environment": noise(streams_of[2], (NTERM, NSEC, M, M), M ** -0.5, 0.21875, ((0, 8), (1, 4))),
        "site_blocks": noise(streams_of[3], (NSEC, M, M), (M ** -0.25), 3.0, ((0, 4),)),
        "sector_sizes": draw_sector_sizes(jax.random.fold_in(streams_of[6], 71), 0),
        "term_shift": touch_ends(jax.random.randint(streams_of[5], (NTERM,), -1, 2), jax.random.fold_in(streams_of[5], 1), -1, 1).astype(jnp.int32),
    }


def shifted(padded, charge_shift):
    return lax.dynamic_slice_in_dim(padded, (charge_shift + 1).astype(jnp.int32), NSEC, 0)


def reference(state, left_environment, right_environment, site_blocks, sector_sizes, term_shift):
    row_index = jnp.arange(M, dtype=jnp.int32)
    valid_rows = (row_index[None, :] < sector_sizes[:, None]).astype(jnp.float32)
    both = valid_rows[:, :, None] * valid_rows[:, None, :]
    masked_state = state.astype(jnp.float32) * both
    masked_site = site_blocks.astype(jnp.float32) * both
    empty = jnp.zeros((1, M, M), jnp.float32)
    state_padded = jnp.concatenate([empty, masked_state, empty], axis=0)
    site_padded = jnp.concatenate([empty, masked_site, empty], axis=0)
    valid_padded = jnp.concatenate([jnp.zeros((1, M), jnp.float32), valid_rows, jnp.zeros((1, M), jnp.float32)], axis=0)
    highest = lax.Precision.HIGHEST

    def one_term(total, inputs):
        left_term, right_term, charge_shift = inputs
        source_valid = shifted(valid_padded, charge_shift)
        source_state = shifted(state_padded, charge_shift)
        source_site = shifted(site_padded, charge_shift)
        left_masked = left_term.astype(jnp.float32) * valid_rows[:, :, None] * source_valid[:, None, :]
        right_masked = right_term.astype(jnp.float32) * source_valid[:, :, None] * valid_rows[:, None, :]
        mixed_block = jnp.einsum("sij,sjk->sik", source_state, right_masked, precision=highest)
        mixed_block = mixed_block.astype(jnp.bfloat16).astype(jnp.float32)
        partial_rows = jnp.einsum("sij,sjk->sik", left_masked, mixed_block, precision=highest)
        carried = jnp.einsum("sij,sjk->sik", left_masked, source_site, precision=highest)
        carried = carried.astype(jnp.bfloat16).astype(jnp.float32)
        renewed = jnp.einsum("sji,sjk->sik", masked_site, carried, precision=highest).astype(jnp.bfloat16)
        return total + partial_rows, renewed

    applied, new_left = lax.scan(one_term, jnp.zeros((NSEC, M, M), jnp.float32), (left_environment, right_environment, term_shift))
    return applied, new_left
```

```python
import functools

import jax
import jax.numpy as jnp
from jax import lax
from jax.experimental import pallas as pl
from jax.experimental.pallas import tpu as pltpu
from jax.sharding import PartitionSpec as P

MESH = pl.DeviceIdType.MESH
BF16 = jnp.bfloat16
F32 = jnp.float32


def flip_bits(number, bits, count):
    out, bit = 0, 1
    while bit < count:
        here = (number // bit) % 2
        out = out + bit * (((here + 1) % 2) if bits & bit else here)
        bit *= 2
    return out


def kernel(
    terms, sectors,
    state, left, right, site, sizes, shift,
    applied, new_left,
    own_s, own_b, lm, rm, mate_s, far_s, mate_b, far_b, bt, mixed, carried,
    kept, y_send, y_recv, z_send, z_recv,
    local_sem, mate_send, mate_recv, x_send_sem, x_recv_sem, relay_send, relay_recv,
    y_send_sem, y_recv_sem, z_send_sem, z_recv_sem,
):
    width = own_s.shape[0]
    depth = terms // 2
    rows = width // terms
    quarter = width // 4
    chunk = quarter // 2
    t, p = lax.axis_index("term"), lax.axis_index("sec")
    z, y = t // 2, t % 2
    odd = p % 2
    mate = p + 1 - 2 * odd
    far = p - 1 + 2 * odd
    has_far = jnp.logical_and(far >= 0, far < sectors)
    far_there = lax.rem(far + sectors, sectors)
    zlow = z % 2
    y_peer = 2 * z + 1 - y
    z_near = 2 * (z + 1 - 2 * zlow) + y
    z_other = [flip_bits(z, depth - 1 - k, depth) for k in range(depth)]

    loads = [
        pltpu.make_async_copy(state.at[0], own_s, local_sem.at[0]),
        pltpu.make_async_copy(left.at[0, 0], lm, local_sem.at[1]),
        pltpu.make_async_copy(right.at[0, 0], rm, local_sem.at[2]),
        pltpu.make_async_copy(site.at[0], own_b, local_sem.at[3]),
    ]
    for load in loads:
        load.start()

    barrier = pltpu.get_barrier_semaphore()
    pl.semaphore_signal(barrier, inc=1, device_id=(t, mate), device_id_type=MESH)

    @pl.when(has_far)
    def _():
        pl.semaphore_signal(barrier, inc=1, device_id=(t, far_there), device_id_type=MESH)

    pl.semaphore_signal(barrier, inc=1, device_id=(y_peer, p), device_id_type=MESH)
    for k in range(depth - 1):
        pl.semaphore_signal(
            barrier, inc=1, device_id=(2 * z_other[k] + y, p), device_id_type=MESH
        )
    pl.semaphore_wait(barrier, depth + 1 + jnp.where(has_far, 1, 0))

    def remote(src, dst, send, recv, device):
        return pltpu.make_async_remote_copy(
            src_ref=src, dst_ref=dst, send_sem=send, recv_sem=recv,
            device_id=device, device_id_type=MESH,
        )

    def part(number, piece=None):
        if piece is None:
            return pl.ds(pl.multiple_of(number * quarter, quarter), quarter)
        return pl.ds(pl.multiple_of(number * quarter + piece * chunk, chunk), chunk)

    q_own = 2 * zlow + y
    q_y = 2 * zlow + 1 - y
    q_z = 2 * (1 - zlow) + y
    q_d = 2 * (1 - zlow) + 1 - y
    there = (t, far_there)
    x_copies = [
        remote(
            state.at[0, part(q_own, i)], far_s.at[part(q_own, i)],
            x_send_sem.at[i], x_recv_sem.at[i], there,
        )
        for i in range(2)
    ]
    x_copies.append(
        remote(
            state.at[0, part(q_d)], far_s.at[part(q_d)],
            x_send_sem.at[2], x_recv_sem.at[2], there,
        )
    )
    x_copies.append(
        remote(site.at[0], far_b, x_send_sem.at[3], x_recv_sem.at[3], there)
    )
    y_relays = [
        remote(
            far_s.at[part(q_own, i)], far_s.at[part(q_own, i)],
            relay_send.at[i], relay_recv.at[i], (y_peer, p),
        )
        for i in range(2)
    ]
    z_relays = [
        remote(
            far_s.at[part(q_own, i)], far_s.at[part(q_own, i)],
            relay_send.at[2 + i], relay_recv.at[2 + i], (z_near, p),
        )
        for i in range(2)
    ]
    y_arrivals = [
        remote(
            far_s.at[part(q_y, i)], far_s.at[part(q_y, i)],
            relay_send.at[i], relay_recv.at[i], (y_peer, p),
        )
        for i in range(2)
    ]
    z_arrivals = [
        remote(
            far_s.at[part(q_z, i)], far_s.at[part(q_z, i)],
            relay_send.at[2 + i], relay_recv.at[2 + i], (z_near, p),
        )
        for i in range(2)
    ]
    mate_copies = [
        remote(state.at[0], mate_s, mate_send.at[0], mate_recv.at[0], (t, mate)),
        remote(site.at[0], mate_b, mate_send.at[1], mate_recv.at[1], (t, mate)),
    ]

    @pl.when(has_far)
    def _():
        for copy in x_copies:
            copy.start()

    for copy in mate_copies:
        copy.start()

    @pl.when(jnp.logical_not(has_far))
    def _():
        far_s[...] = jnp.zeros_like(far_s)
        far_b[...] = jnp.zeros_like(far_b)

    charge_shift = shift[0]
    own_size = jnp.int32(0)
    source_size = jnp.int32(0)
    for i in range(sectors):
        own_size = own_size + jnp.where(p == i, sizes[i], 0)
        source_size = source_size + jnp.where(p + charge_shift == i, sizes[i], 0)
    towards = charge_shift * (1 - 2 * odd)

    def choose(own, near, away):
        return jnp.where(towards == 0, own, jnp.where(towards == 1, near, away))

    loads[2].wait()
    row_ids = lax.broadcasted_iota(jnp.int32, (width, 1), 0)
    rm[...] = rm[...] * jnp.where(row_ids < source_size, 1.0, 0.0).astype(BF16)
    loads[1].wait()
    col_ids = lax.broadcasted_iota(jnp.int32, (1, width), 1)
    lm[...] = lm[...] * jnp.where(col_ids < source_size, 1.0, 0.0).astype(BF16)

    @pl.when(has_far)
    def _():
        for i in range(2):
            x_copies[i].wait_recv()
            y_relays[i].start()
            z_relays[i].start()

    loads[3].wait()
    bt[...] = own_b[...].T
    loads[0].wait()
    mate_copies[0].wait_recv()

    def mix(number):
        where = part(number)
        source = choose(own_s[where, :], mate_s[where, :], far_s[where, :])
        mixed[where, :] = jnp.dot(source, rm[...], preferred_element_type=F32).astype(BF16)

    mix(q_own)

    @pl.when(has_far)
    def _():
        x_copies[2].wait_recv()

    mix(q_d)

    @pl.when(has_far)
    def _():
        for copy in y_arrivals:
            copy.wait_recv()

    mix(q_y)

    @pl.when(has_far)
    def _():
        for copy in z_arrivals:
            copy.wait_recv()

    mix(q_z)

    y_copies, z_copies = [], []
    for k in range(depth):
        start = pl.multiple_of(z_other[k] * 2 * rows, 2 * rows)
        give = pl.ds(pl.multiple_of(start + (1 - y) * rows, rows), rows)
        keep = pl.ds(pl.multiple_of(start + y * rows, rows), rows)
        both = jnp.dot(
            jnp.concatenate([lm[give, :], lm[keep, :]], axis=0), mixed[...],
            preferred_element_type=F32,
        )
        y_send[k] = both[:rows].astype(BF16)
        copy = remote(
            y_send.at[k], y_recv.at[k], y_send_sem.at[k], y_recv_sem.at[k], (y_peer, p)
        )
        copy.start()
        y_copies.append(copy)
        kept[k] = both[rows:]

    for k in range(depth - 1):
        y_copies[k].wait_recv()
        z_send[k] = (kept[k] + y_recv[k].astype(F32)).astype(BF16)
        copy = remote(
            z_send.at[k], z_recv.at[k], z_send_sem.at[k], z_recv_sem.at[k],
            (2 * z_other[k] + y, p),
        )
        copy.start()
        z_copies.append(copy)

    mate_copies[1].wait_recv()

    @pl.when(has_far)
    def _():
        x_copies[3].wait_recv()

    own_b[...] = choose(own_b[...], mate_b[...], far_b[...])
    for i in range(4):
        where = pl.ds(i * quarter, quarter)
        carried[where, :] = jnp.dot(
            lm[where, :], own_b[...], preferred_element_type=F32
        ).astype(BF16)
    row_part = lax.broadcasted_iota(jnp.int32, (width, 1), 0)
    lane_mask = (col_ids < source_size).astype(F32)
    carried[...] = carried[...] * jnp.where(row_part < own_size, 1.0, 0.0).astype(BF16)
    for i in range(4):
        where = pl.ds(i * quarter, quarter)
        renewed = jnp.dot(bt[where, :], carried[...], preferred_element_type=F32)
        ids = lax.broadcasted_iota(jnp.int32, (quarter, 1), 0) + i * quarter
        renewed = renewed * lane_mask * (ids < own_size).astype(F32)
        new_left[0, 0, where, :] = renewed.astype(BF16)

    last = depth - 1
    y_copies[last].wait_recv()
    total = kept[last] + y_recv[last].astype(F32)
    for k in range(depth - 1):
        z_copies[k].wait_recv()
        total = total + z_recv[k].astype(F32)
    ids = lax.broadcasted_iota(jnp.int32, (rows, 1), 0) + t * rows
    keep_rows = (ids < own_size).astype(F32)
    keep_cols = (col_ids < own_size).astype(F32)
    applied[0] = total * keep_rows * keep_cols

    for copy in y_copies + z_copies + mate_copies:
        copy.wait_send()

    @pl.when(has_far)
    def _():
        for copy in x_copies + y_relays + z_relays:
            copy.wait_send()


def shards(terms, sectors, state, left_environment, right_environment, site_blocks,
           sector_sizes, term_shift):
    width = state.shape[1]
    rows = width // terms
    depth = terms // 2
    square = pltpu.VMEM((width, width), BF16)
    any_space = pl.BlockSpec(memory_space=pl.ANY)
    smem = pl.BlockSpec(memory_space=pltpu.SMEM)
    vmem = pl.BlockSpec(memory_space=pltpu.VMEM)
    dma = pltpu.SemaphoreType.DMA
    return pl.pallas_call(
        functools.partial(kernel, terms, sectors),
        out_shape=(
            jax.ShapeDtypeStruct((1, rows, width), F32),
            jax.ShapeDtypeStruct((1, 1, width, width), BF16),
        ),
        in_specs=[any_space] * 4 + [smem] * 2,
        out_specs=(vmem, vmem),
        scratch_shapes=[square] * 11 + [
            pltpu.VMEM((depth, rows, width), F32),
            pltpu.VMEM((depth, rows, width), BF16),
            pltpu.VMEM((depth, rows, width), BF16),
            pltpu.VMEM((depth, rows, width), BF16),
            pltpu.VMEM((depth, rows, width), BF16),
            dma((4,)), dma((2,)), dma((2,)), dma((4,)), dma((4,)), dma((4,)), dma((4,)),
            dma((depth,)), dma((depth,)), dma((depth,)), dma((depth,)),
        ],
        compiler_params=pltpu.CompilerParams(
            collective_id=0, has_side_effects=True, vmem_limit_bytes=48 * 1024 * 1024
        ),
    )(state, left_environment, right_environment, site_blocks, sector_sizes, term_shift)


def solution(mesh):
    placed = (
        P("sec", None, None),
        P("term", "sec", None, None),
        P("term", "sec", None, None),
        P("sec", None, None),
        P(),
        P("term"),
    )
    return jax.shard_map(
        functools.partial(shards, mesh.shape["term"], mesh.shape["sec"]),
        mesh=mesh,
        in_specs=placed,
        out_specs=(P("sec", "term", None), P("term", "sec", None, None)),
        check_vma=False,
    )
```

```python
import functools

import jax
import jax.numpy as jnp
from jax import lax
from jax.experimental import pallas as pl
from jax.experimental.pallas import tpu as pltpu
from jax.sharding import PartitionSpec as P

MESH = pl.DeviceIdType.MESH
BF16 = jnp.bfloat16
F32 = jnp.float32


def flip_bits(number, bits, count):
    out, bit = 0, 1
    while bit < count:
        here = (number // bit) % 2
        out = out + bit * (((here + 1) % 2) if bits & bit else here)
        bit *= 2
    return out


def kernel(
    terms, sectors,
    state, left, right, site, sizes_there, shift_there,
    applied, new_left,
    own_s, own_b, lm, rm, mate_s, far_s, mate_b, far_b, bt, mixed, carried,
    kept, y_send, y_recv, z_send, z_recv,
    sizes, shift, local_sem, mate_send, mate_recv, x_send_sem, x_recv_sem, relay_send, relay_recv,
    y_send_sem, y_recv_sem, z_send_sem, z_recv_sem,
):
    width = own_s.shape[0]
    depth = terms // 2
    rows = width // terms
    quarter = width // 4
    chunk = quarter // 2
    t, p = lax.axis_index("term"), lax.axis_index("sec")
    z, y = t // 2, t % 2
    odd = p % 2
    mate = p + 1 - 2 * odd
    far = p - 1 + 2 * odd
    has_far = jnp.logical_and(far >= 0, far < sectors)
    far_there = lax.rem(far + sectors, sectors)
    zlow = z % 2
    y_peer = 2 * z + 1 - y
    z_near = 2 * (z + 1 - 2 * zlow) + y
    z_other = [flip_bits(z, depth - 1 - k, depth) for k in range(depth)]

    loads = [
        pltpu.make_async_copy(state.at[0], own_s, local_sem.at[0]),
        pltpu.make_async_copy(left.at[0, 0], lm, local_sem.at[1]),
        pltpu.make_async_copy(right.at[0, 0], rm, local_sem.at[2]),
        pltpu.make_async_copy(site.at[0], own_b, local_sem.at[3]),
        pltpu.make_async_copy(sizes_there, sizes, local_sem.at[4]),
        pltpu.make_async_copy(shift_there, shift, local_sem.at[5]),
    ]
    for load in loads:
        load.start()

    barrier = pltpu.get_barrier_semaphore()
    pl.semaphore_signal(barrier, inc=1, device_id=(t, mate), device_id_type=MESH)

    @pl.when(has_far)
    def _():
        pl.semaphore_signal(barrier, inc=1, device_id=(t, far_there), device_id_type=MESH)

    pl.semaphore_signal(barrier, inc=1, device_id=(y_peer, p), device_id_type=MESH)
    for k in range(depth - 1):
        pl.semaphore_signal(
            barrier, inc=1, device_id=(2 * z_other[k] + y, p), device_id_type=MESH
        )
    pl.semaphore_wait(barrier, depth + 1 + jnp.where(has_far, 1, 0))

    def remote(src, dst, send, recv, device):
        return pltpu.make_async_remote_copy(
            src_ref=src, dst_ref=dst, send_sem=send, recv_sem=recv,
            device_id=device, device_id_type=MESH,
        )

    def part(number, piece=None):
        if piece is None:
            return pl.ds(pl.multiple_of(number * quarter, quarter), quarter)
        return pl.ds(pl.multiple_of(number * quarter + piece * chunk, chunk), chunk)

    q_own = 2 * zlow + y
    q_y = 2 * zlow + 1 - y
    q_z = 2 * (1 - zlow) + y
    q_d = 2 * (1 - zlow) + 1 - y
    there = (t, far_there)
    x_copies = [
        remote(
            state.at[0, part(q_own, i)], far_s.at[part(q_own, i)],
            x_send_sem.at[i], x_recv_sem.at[i], there,
        )
        for i in range(2)
    ]
    x_copies.append(
        remote(
            state.at[0, part(q_d)], far_s.at[part(q_d)],
            x_send_sem.at[2], x_recv_sem.at[2], there,
        )
    )
    x_copies.append(
        remote(site.at[0], far_b, x_send_sem.at[3], x_recv_sem.at[3], there)
    )
    y_relays = [
        remote(
            far_s.at[part(q_own, i)], far_s.at[part(q_own, i)],
            relay_send.at[i], relay_recv.at[i], (y_peer, p),
        )
        for i in range(2)
    ]
    z_relays = [
        remote(
            far_s.at[part(q_own, i)], far_s.at[part(q_own, i)],
            relay_send.at[2 + i], relay_recv.at[2 + i], (z_near, p),
        )
        for i in range(2)
    ]
    y_arrivals = [
        remote(
            far_s.at[part(q_y, i)], far_s.at[part(q_y, i)],
            relay_send.at[i], relay_recv.at[i], (y_peer, p),
        )
        for i in range(2)
    ]
    z_arrivals = [
        remote(
            far_s.at[part(q_z, i)], far_s.at[part(q_z, i)],
            relay_send.at[2 + i], relay_recv.at[2 + i], (z_near, p),
        )
        for i in range(2)
    ]
    mate_copies = [
        remote(state.at[0], mate_s, mate_send.at[0], mate_recv.at[0], (t, mate)),
        remote(site.at[0], mate_b, mate_send.at[1], mate_recv.at[1], (t, mate)),
    ]

    @pl.when(has_far)
    def _():
        for copy in x_copies:
            copy.start()

    for copy in mate_copies:
        copy.start()

    @pl.when(jnp.logical_not(has_far))
    def _():
        far_s[...] = jnp.zeros_like(far_s)
        far_b[...] = jnp.zeros_like(far_b)

    loads[4].wait()
    loads[5].wait()
    charge_shift = shift[0]
    own_size = jnp.int32(0)
    source_size = jnp.int32(0)
    for i in range(sectors):
        own_size = own_size + jnp.where(p == i, sizes[i], 0)
        source_size = source_size + jnp.where(p + charge_shift == i, sizes[i], 0)
    towards = charge_shift * (1 - 2 * odd)

    def choose(own, near, away):
        return jnp.where(towards == 0, own, jnp.where(towards == 1, near, away))

    loads[2].wait()
    row_ids = lax.broadcasted_iota(jnp.int32, (width, 1), 0)
    rm[...] = rm[...] * jnp.where(row_ids < source_size, 1.0, 0.0).astype(BF16)
    loads[1].wait()
    col_ids = lax.broadcasted_iota(jnp.int32, (1, width), 1)
    lm[...] = lm[...] * jnp.where(col_ids < source_size, 1.0, 0.0).astype(BF16)

    @pl.when(has_far)
    def _():
        for i in range(2):
            x_copies[i].wait_recv()
            y_relays[i].start()
            z_relays[i].start()

    loads[3].wait()
    bt[...] = own_b[...].T
    loads[0].wait()
    mate_copies[0].wait_recv()

    def mix(number):
        where = part(number)
        source = choose(own_s[where, :], mate_s[where, :], far_s[where, :])
        mixed[where, :] = jnp.dot(source, rm[...], preferred_element_type=F32).astype(BF16)

    mix(q_own)

    @pl.when(has_far)
    def _():
        x_copies[2].wait_recv()

    mix(q_d)

    @pl.when(has_far)
    def _():
        for copy in y_arrivals:
            copy.wait_recv()

    mix(q_y)

    @pl.when(has_far)
    def _():
        for copy in z_arrivals:
            copy.wait_recv()

    mix(q_z)

    y_copies, z_copies = [], []
    for k in range(depth):
        start = pl.multiple_of(z_other[k] * 2 * rows, 2 * rows)
        give = pl.ds(pl.multiple_of(start + (1 - y) * rows, rows), rows)
        keep = pl.ds(pl.multiple_of(start + y * rows, rows), rows)
        both = jnp.dot(
            jnp.concatenate([lm[give, :], lm[keep, :]], axis=0), mixed[...],
            preferred_element_type=F32,
        )
        y_send[k] = both[:rows].astype(BF16)
        copy = remote(
            y_send.at[k], y_recv.at[k], y_send_sem.at[k], y_recv_sem.at[k], (y_peer, p)
        )
        copy.start()
        y_copies.append(copy)
        kept[k] = both[rows:]

    for k in range(depth - 1):
        y_copies[k].wait_recv()
        z_send[k] = (kept[k] + y_recv[k].astype(F32)).astype(BF16)
        copy = remote(
            z_send.at[k], z_recv.at[k], z_send_sem.at[k], z_recv_sem.at[k],
            (2 * z_other[k] + y, p),
        )
        copy.start()
        z_copies.append(copy)

    mate_copies[1].wait_recv()

    @pl.when(has_far)
    def _():
        x_copies[3].wait_recv()

    own_b[...] = choose(own_b[...], mate_b[...], far_b[...])
    for i in range(4):
        where = pl.ds(i * quarter, quarter)
        carried[where, :] = jnp.dot(
            lm[where, :], own_b[...], preferred_element_type=F32
        ).astype(BF16)
    row_part = lax.broadcasted_iota(jnp.int32, (width, 1), 0)
    lane_mask = (col_ids < source_size).astype(F32)
    carried[...] = carried[...] * jnp.where(row_part < own_size, 1.0, 0.0).astype(BF16)
    for i in range(4):
        where = pl.ds(i * quarter, quarter)
        renewed = jnp.dot(bt[where, :], carried[...], preferred_element_type=F32)
        ids = lax.broadcasted_iota(jnp.int32, (quarter, 1), 0) + i * quarter
        renewed = renewed * lane_mask * (ids < own_size).astype(F32)
        new_left[0, 0, where, :] = renewed.astype(BF16)

    last = depth - 1
    y_copies[last].wait_recv()
    total = kept[last] + y_recv[last].astype(F32)
    for k in range(depth - 1):
        z_copies[k].wait_recv()
        total = total + z_recv[k].astype(F32)
    ids = lax.broadcasted_iota(jnp.int32, (rows, 1), 0) + t * rows
    keep_rows = (ids < own_size).astype(F32)
    keep_cols = (col_ids < own_size).astype(F32)
    applied[0] = total * keep_rows * keep_cols

    for copy in y_copies + z_copies + mate_copies:
        copy.wait_send()

    @pl.when(has_far)
    def _():
        for copy in x_copies + y_relays + z_relays:
            copy.wait_send()


def shards(terms, sectors, state, left_environment, right_environment, site_blocks,
           sector_sizes, term_shift):
    width = state.shape[1]
    rows = width // terms
    depth = terms // 2
    square = pltpu.VMEM((width, width), BF16)
    hbm = pl.BlockSpec(memory_space=pltpu.HBM)
    vmem = pl.BlockSpec(memory_space=pltpu.VMEM)
    dma = pltpu.SemaphoreType.DMA
    return pl.pallas_call(
        functools.partial(kernel, terms, sectors),
        out_shape=(
            pltpu.VMEM((1, rows, width), F32),
            pltpu.VMEM((1, 1, width, width), BF16),
        ),
        in_specs=[hbm] * 6,
        out_specs=(vmem, vmem),
        scratch_shapes=[square] * 11 + [
            pltpu.VMEM((depth, rows, width), F32),
            pltpu.VMEM((depth, rows, width), BF16),
            pltpu.VMEM((depth, rows, width), BF16),
            pltpu.VMEM((depth, rows, width), BF16),
            pltpu.VMEM((depth, rows, width), BF16),
            pltpu.SMEM((sectors,), jnp.int32), pltpu.SMEM((1,), jnp.int32),
            dma((6,)), dma((2,)), dma((2,)), dma((4,)), dma((4,)), dma((4,)), dma((4,)),
            dma((depth,)), dma((depth,)), dma((depth,)), dma((depth,)),
        ],
        compiler_params=pltpu.CompilerParams(
            collective_id=0, has_side_effects=True, vmem_limit_bytes=62500 * 1024
        ),
    )(state, left_environment, right_environment, site_blocks, sector_sizes, term_shift)


def solution(mesh):
    placed = (
        P("sec", None, None),
        P("term", "sec", None, None),
        P("term", "sec", None, None),
        P("sec", None, None),
        P(),
        P("term"),
    )
    return jax.shard_map(
        functools.partial(shards, mesh.shape["term"], mesh.shape["sec"]),
        mesh=mesh,
        in_specs=placed,
        out_specs=(P("sec", "term", None), P("term", "sec", None, None)),
        check_vma=False,
    )
```

```python
import functools

import jax
import jax.numpy as jnp
from jax import lax
from jax.experimental import pallas as pl
from jax.experimental.pallas import tpu as pltpu
from jax.sharding import PartitionSpec as P

MESH = pl.DeviceIdType.MESH
BF16 = jnp.bfloat16
F32 = jnp.float32


def flip_bits(number, bits, count):
    out, bit = 0, 1
    while bit < count:
        here = (number // bit) % 2
        out = out + bit * (((here + 1) % 2) if bits & bit else here)
        bit *= 2
    return out


def kernel(
    terms, sectors,
    state, left, right, site, sizes_there, shift_there,
    applied, new_left,
    own_s, own_b, lm, rm, mate_s, far_s, mate_b, far_b, bt, mixed, weight,
    acc, kept, y_send, y_recv, z_send, z_recv,
    sizes, shift, local_sem, mate_send, mate_recv, x_send_sem, x_recv_sem, relay_send, relay_recv,
    y_send_sem, y_recv_sem, z_send_sem, z_recv_sem,
):
    width = own_s.shape[0]
    depth = terms // 2
    rows = width // terms
    quarter = width // 4
    chunk = quarter // 2
    t, p = lax.axis_index("term"), lax.axis_index("sec")
    z, y = t // 2, t % 2
    odd = p % 2
    mate = p + 1 - 2 * odd
    far = p - 1 + 2 * odd
    has_far = jnp.logical_and(far >= 0, far < sectors)
    far_there = lax.rem(far + sectors, sectors)
    zlow = z % 2
    y_peer = 2 * z + 1 - y
    z_near = 2 * (z + 1 - 2 * zlow) + y
    even = [h for h in range(1, depth) if bin(h).count("1") % 2 == 0]
    order = [1 ^ h for h in even] + [1] + even + [0]
    z_other = [flip_bits(z, mask, depth) for mask in order]
    neighbours = len(even) + 1

    loads = [
        pltpu.make_async_copy(state.at[0], own_s, local_sem.at[0]),
        pltpu.make_async_copy(left.at[0, 0], lm, local_sem.at[1]),
        pltpu.make_async_copy(right.at[0, 0], rm, local_sem.at[2]),
        pltpu.make_async_copy(site.at[0], own_b, local_sem.at[3]),
        pltpu.make_async_copy(sizes_there, sizes, local_sem.at[4]),
        pltpu.make_async_copy(shift_there, shift, local_sem.at[5]),
    ]
    for load in loads:
        load.start()

    barrier = pltpu.get_barrier_semaphore()
    pl.semaphore_signal(barrier, inc=1, device_id=(t, mate), device_id_type=MESH)

    @pl.when(has_far)
    def _():
        pl.semaphore_signal(barrier, inc=1, device_id=(t, far_there), device_id_type=MESH)

    pl.semaphore_signal(barrier, inc=1, device_id=(y_peer, p), device_id_type=MESH)
    for k in range(neighbours - 1, depth - 1):
        pl.semaphore_signal(
            barrier, inc=1, device_id=(2 * z_other[k] + y, p), device_id_type=MESH
        )

    @pl.when(jnp.logical_not(has_far))
    def _():
        far_s[...] = jnp.zeros_like(far_s)
        far_b[...] = jnp.zeros_like(far_b)

    pl.semaphore_wait(barrier, neighbours + 2 + jnp.where(has_far, 1, 0))

    def remote(src, dst, send, recv, device):
        return pltpu.make_async_remote_copy(
            src_ref=src, dst_ref=dst, send_sem=send, recv_sem=recv,
            device_id=device, device_id_type=MESH,
        )

    def part(number, piece=None):
        if piece is None:
            return pl.ds(pl.multiple_of(number * quarter, quarter), quarter)
        return pl.ds(pl.multiple_of(number * quarter + piece * chunk, chunk), chunk)

    q_own = 2 * zlow + y
    q_y = 2 * zlow + 1 - y
    q_z = 2 * (1 - zlow) + y
    q_d = 2 * (1 - zlow) + 1 - y
    there = (t, far_there)
    x_copies = [
        remote(
            state.at[0, part(q_own, i)], far_s.at[part(q_own, i)],
            x_send_sem.at[i], x_recv_sem.at[i], there,
        )
        for i in range(2)
    ]
    x_copies.append(
        remote(
            state.at[0, part(q_d)], far_s.at[part(q_d)],
            x_send_sem.at[2], x_recv_sem.at[2], there,
        )
    )
    x_state = remote(
        state.at[0, part(q_y, 1)], far_s.at[part(q_y, 1)],
        x_send_sem.at[5], x_recv_sem.at[5], there,
    )
    late = 2 * (width // 3)
    site_parts = [pl.ds(0, late), pl.ds(late, width - late)]
    for i, rows_of in enumerate(site_parts):
        x_copies.append(
            remote(
                site.at[0, rows_of], far_b.at[rows_of],
                x_send_sem.at[3 + i], x_recv_sem.at[3 + i], there,
            )
        )
    y_relays = [
        remote(
            far_s.at[part(q_own, i)], far_s.at[part(q_own, i)],
            relay_send.at[i], relay_recv.at[i], (y_peer, p),
        )
        for i in range(1)
    ]
    z_relays = [
        remote(
            far_s.at[part(q_own, i)], far_s.at[part(q_own, i)],
            relay_send.at[2 + i], relay_recv.at[2 + i], (z_near, p),
        )
        for i in range(2)
    ]
    y_arrivals = [
        remote(
            far_s.at[part(q_y, i)], far_s.at[part(q_y, i)],
            relay_send.at[i], relay_recv.at[i], (y_peer, p),
        )
        for i in range(1)
    ]
    z_arrivals = [
        remote(
            far_s.at[part(q_z, i)], far_s.at[part(q_z, i)],
            relay_send.at[2 + i], relay_recv.at[2 + i], (z_near, p),
        )
        for i in range(2)
    ]
    mate_copies = [
        remote(
            state.at[0, part(q)], mate_s.at[part(q)], mate_send.at[i], mate_recv.at[i],
            (t, mate),
        )
        for i, q in enumerate((q_own, q_d, q_y, q_z))
    ]
    mate_site = remote(site.at[0], mate_b, mate_send.at[4], mate_recv.at[4], (t, mate))

    @pl.when(has_far)
    def _():
        for copy in x_copies[:3] + [x_state] + x_copies[3:]:
            copy.start()

    for copy in mate_copies:
        copy.start()

    loads[4].wait()
    loads[5].wait()
    charge_shift = shift[0]
    own_size = jnp.int32(0)
    source_size = jnp.int32(0)
    for i in range(sectors):
        own_size = own_size + jnp.where(p == i, sizes[i], 0)
        source_size = source_size + jnp.where(p + charge_shift == i, sizes[i], 0)
    towards = charge_shift * (1 - 2 * odd)

    def choose(own, near, away):
        return jnp.where(towards == 0, own, jnp.where(towards == 1, near, away))

    loads[2].wait()
    row_ids = lax.broadcasted_iota(jnp.int32, (width, 1), 0)
    rm[...] = rm[...] * jnp.where(row_ids < source_size, 1.0, 0.0).astype(BF16)
    loads[1].wait()
    col_ids = lax.broadcasted_iota(jnp.int32, (1, width), 1)
    lm[...] = lm[...] * jnp.where(col_ids < source_size, 1.0, 0.0).astype(BF16)

    @pl.when(has_far)
    def _():
        for i in range(2):
            x_copies[i].wait_recv()
            if i == 0:
                y_relays[i].start()
            z_relays[i].start()

    loads[0].wait()
    def mix(i, number):
        mate_copies[i].wait_recv()
        where = part(number)
        source = choose(own_s[where, :], mate_s[where, :], far_s[where, :])
        mixed[where, :] = jnp.dot(source, rm[...], preferred_element_type=F32).astype(BF16)

    mix(0, q_own)

    @pl.when(has_far)
    def _():
        x_copies[2].wait_recv()

    mix(1, q_d)

    @pl.when(has_far)
    def _():
        x_state.wait_recv()
        for copy in y_arrivals:
            copy.wait_recv()

    mix(2, q_y)

    @pl.when(has_far)
    def _():
        for copy in z_arrivals:
            copy.wait_recv()

    mix(3, q_z)
    mate_site.start()

    y_copies, z_copies = [], []
    for k in range(depth):
        start = pl.multiple_of(z_other[k] * 2 * rows, 2 * rows)
        give = pl.ds(pl.multiple_of(start + (1 - y) * rows, rows), rows)
        keep = pl.ds(pl.multiple_of(start + y * rows, rows), rows)
        both = jnp.dot(
            jnp.concatenate([lm[give, :], lm[keep, :]], axis=0), mixed[...],
            preferred_element_type=F32,
        )
        y_send[k] = both[:rows].astype(BF16)
        copy = remote(
            y_send.at[k], y_recv.at[k], y_send_sem.at[k], y_recv_sem.at[k], (y_peer, p)
        )
        copy.start()
        y_copies.append(copy)
        kept[k] = both[rows:]

    loads[3].wait()
    own_rows = (row_ids < own_size).astype(F32)
    bt[...] = (own_b[...] * own_rows.astype(BF16)).T
    for i in range(4):
        where = pl.ds(i * quarter, quarter)
        weight[where, :] = jnp.dot(
            bt[where, :], lm[...], preferred_element_type=F32
        ).astype(BF16)

    for k in range(depth - 1):
        y_copies[k].wait_recv()
        value = kept[k] + y_recv[k].astype(F32)
        if k >= neighbours:
            z_copies[k - neighbours].wait_recv()
            value = value + z_recv[k - neighbours].astype(F32)
        z_send[k] = value.astype(BF16)
        peer = z_near if k < neighbours else 2 * z_other[k] + y
        copy = remote(
            z_send.at[k], z_recv.at[k], z_send_sem.at[k], z_recv_sem.at[k], (peer, p)
        )
        copy.start()
        z_copies.append(copy)

    mate_site.wait_recv()

    @pl.when(has_far)
    def _():
        x_copies[3].wait_recv()

    early = pl.ds(0, late)
    own_b[early, :] = choose(own_b[early, :], mate_b[early, :], far_b[early, :])
    for i in range(4):
        where = pl.ds(i * quarter, quarter)
        acc[where, :] = jnp.dot(
            weight[where, early], own_b[early, :], preferred_element_type=F32
        )

    last = depth - 1
    y_copies[last].wait_recv()
    kept[last] = kept[last] + y_recv[last].astype(F32)

    @pl.when(has_far)
    def _():
        x_copies[4].wait_recv()

    rest = pl.ds(late, width - late)
    lane_mask = (col_ids < source_size).astype(F32)
    tail = choose(own_b[rest, :], mate_b[rest, :], far_b[rest, :])
    for i in range(4):
        where = pl.ds(i * quarter, quarter)
        renewed = acc[where, :] + jnp.dot(
            weight[where, rest], tail, preferred_element_type=F32
        )
        ids = lax.broadcasted_iota(jnp.int32, (quarter, 1), 0) + i * quarter
        renewed = renewed * lane_mask * (ids < own_size).astype(F32)
        new_left[0, 0, where, :] = renewed.astype(BF16)

    total = kept[last]
    for k in range(neighbours - 1, depth - 1):
        z_copies[k].wait_recv()
        total = total + z_recv[k].astype(F32)
    ids = lax.broadcasted_iota(jnp.int32, (rows, 1), 0) + t * rows
    keep_rows = (ids < own_size).astype(F32)
    keep_cols = (col_ids < own_size).astype(F32)
    applied[0] = total * keep_rows * keep_cols

    for copy in y_copies + z_copies + mate_copies + [mate_site]:
        copy.wait_send()

    @pl.when(has_far)
    def _():
        for copy in x_copies + [x_state] + y_relays + z_relays:
            copy.wait_send()


def shards(terms, sectors, state, left_environment, right_environment, site_blocks,
           sector_sizes, term_shift):
    width = state.shape[1]
    rows = width // terms
    depth = terms // 2
    square = pltpu.VMEM((width, width), BF16)
    hbm = pl.BlockSpec(memory_space=pltpu.HBM)
    vmem = pl.BlockSpec(memory_space=pltpu.VMEM)
    dma = pltpu.SemaphoreType.DMA
    return pl.pallas_call(
        functools.partial(kernel, terms, sectors),
        out_shape=(
            pltpu.VMEM((1, rows, width), F32),
            pltpu.VMEM((1, 1, width, width), BF16),
        ),
        in_specs=[hbm] * 6,
        out_specs=(vmem, vmem),
        scratch_shapes=[square] * 11 + [
            pltpu.VMEM((width, width), F32),
            pltpu.VMEM((depth, rows, width), F32),
            pltpu.VMEM((depth, rows, width), BF16),
            pltpu.VMEM((depth, rows, width), BF16),
            pltpu.VMEM((depth, rows, width), BF16),
            pltpu.VMEM((depth, rows, width), BF16),
            pltpu.SMEM((sectors,), jnp.int32), pltpu.SMEM((1,), jnp.int32),
            dma((6,)), dma((5,)), dma((5,)), dma((6,)), dma((6,)), dma((4,)), dma((4,)),
            dma((depth,)), dma((depth,)), dma((depth,)), dma((depth,)),
        ],
        compiler_params=pltpu.CompilerParams(
            collective_id=0, has_side_effects=True, vmem_limit_bytes=62500 * 1024
        ),
    )(state, left_environment, right_environment, site_blocks, sector_sizes, term_shift)


def solution(mesh):
    placed = (
        P("sec", None, None),
        P("term", "sec", None, None),
        P("term", "sec", None, None),
        P("sec", None, None),
        P(),
        P("term"),
    )
    return jax.shard_map(
        functools.partial(shards, mesh.shape["term"], mesh.shape["sec"]),
        mesh=mesh,
        in_specs=placed,
        out_specs=(P("sec", "term", None), P("term", "sec", None, None)),
        check_vma=False,
    )
```
